128 devices in a mesh: row: 8 (over y_lo, x), col: 16 (over z, y_hi, core).
Axes of the slice: x: 4, y: 4 (y_hi: 2, y_lo: 2; y = y_hi * 2 + y_lo), z: 4, core: 2. Of those that a mesh axis runs over, the one named last changes fastest.
Arguments:
- points: bfloat16 [64, 65536], P(None, ('row', 'col')), may hold values from -6 to 6
- solution: float32 [16, 65536], P(None, ('row', 'col')), may hold values from -6 to 6
- residual: float32 [16, 65536], P(None, ('row', 'col')), may hold values from -6 to 6
- direction: float32 [16, 65536], P(None, ('row', 'col')), may hold values from -6 to 6
Outputs:
- solution_next: float32 [16, 65536], P(None, ('row', 'col'))
- residual_next: float32 [16, 65536], P(None, ('row', 'col'))
- direction_next: float32 [16, 65536], P(None, ('row', 'col'))
The draws below stay inside these ranges and needn't reach their ends.
All inputs are finite; a program needn't handle non-finite values.
Results may differ from the reference program's by a relative error of at most 0.0042.
Values may be sent and summed in bfloat16 or wider, within the bound.
A program may use at most 64 MiB of HBM per device.

```python
import jax
import jax.numpy as jnp
from jax import lax

F = 64
R = 16
TILE = 2048
N = 65536


def levels(own_key, dims, split, least, top_value):
    gain, own = 1.0, jax.random.fold_in(own_key, 6)
    for axis_at, blocks in split:
        heights = jnp.exp(jax.random.uniform(jax.random.fold_in(own, axis_at), (blocks,), jnp.float32, least / len(split), top_value / len(split)))
        gain = gain * jnp.repeat(heights, dims[axis_at] // blocks).reshape([-1 if axis == axis_at else 1 for axis in range(len(dims))])
    return gain


def scatter_about(rng, dims, scale, most, shards=(), dtype=jnp.bfloat16):
    entries = jax.random.normal(rng, dims, jnp.float32) * scale
    if len(shards) > 0:
        entries = levels(rng, dims, shards, -0.22, 0.18) * entries
    return jnp.clip(entries, min=-most, max=most).astype(dtype)


def setup_inputs(seed: int = 0) -> dict:
    splits = jax.random.split(jax.random.key(seed), 5)
    points = scatter_about(splits[0], (F, N), 1.0, 6.0, ((1, 128),))
    solution = scatter_about(splits[1], (R, N), 1.0, 6.0, ((1, 128),), jnp.float32)
    residual = scatter_about(splits[2], (R, N), 1.0, 6.0, ((1, 128),), jnp.float32)
    direction = scatter_about(splits[3], (R, N), 1.0, 6.0, ((1, 128),), jnp.float32)
    return dict(points=points, solution=solution, residual=residual, direction=direction)


def reference(points, solution, residual, direction):
    features = points.shape[0]
    total_points = points.shape[1]
    block_rows = min(512, TILE)
    point_f = points.astype(jnp.float32)
    sq_norms = jnp.sum(point_f * point_f, axis=0)
    dir_b = direction.astype(jnp.bfloat16)

    def kernel_rows(row_start):
        row_points = lax.dynamic_slice_in_dim(points, row_start, block_rows, 1)
        row_norms = lax.dynamic_slice_in_dim(sq_norms, row_start, block_rows, 0)
        cross_terms = lax.dot_general(row_points, points, (((0,), (0,)), ((), ())), preferred_element_type=jnp.float32)
        dist = row_norms[:, None] + sq_norms[None, :] - 2.0 * cross_terms
        kernel = jnp.exp(-(2.0 / features) * dist).astype(jnp.bfloat16)
        return lax.dot_general(dir_b, kernel, (((1,), (1,)), ((), ())), preferred_element_type=jnp.float32)

    starts = (jnp.arange(total_points // block_rows) * block_rows).astype(jnp.int32)
    blocks = lax.map(kernel_rows, starts)
    kp = jnp.transpose(blocks, (1, 0, 2)).reshape(direction.shape[0], total_points)
    image = 1.0 * direction + kp
    old_norm = jnp.sum(residual * residual, axis=1)
    curvature = jnp.sum(direction * image, axis=1)
    step_size = old_norm / curvature
    solution_next = solution + step_size[:, None] * direction
    residual_next = residual - step_size[:, None] * image
    new_norm = jnp.sum(residual_next * residual_next, axis=1)
    direction_next = residual_next + (new_norm / old_norm)[:, None] * direction
    return (solution_next, residual_next, direction_next)
```

```python
import math

import jax
import jax.numpy as jnp
from jax import lax
from jax.experimental import pallas as pl
from jax.experimental.pallas import tpu as pltpu
from jax.sharding import PartitionSpec as P

OWN = ((0, 0), (0, 1), (1, 0), (1, 1), (3, 0), (3, 1), (2, 0), (2, 1))
PARTNER = ((0, 0), (0, 1), (3, 0), (3, 1), (2, 0), (2, 1), (1, 0), (1, 1))
F, R, W = 64, 16, 512
DEPTH = F + 16
ROWS = DEPTH + R
GROUPS = 16
MESH = pl.DeviceIdType.MESH
bf16, f32 = jnp.bfloat16, jnp.float32


def place(group, x, core):
    y, z = lax.div(group, 4), lax.rem(group, 4)
    return (lax.rem(y, 2) * 4 + x, z * 4 + lax.div(y, 2) * 2 + core)


def step_kernel(points, residual, direction, image, coefs, blk, lhs, acc, kbuf, rs, stat, st1, st2,
                g_send, g_recv, r_send, r_recv, a_send, a_recv, b_send, b_recv):
    row, col = lax.axis_index("row"), lax.axis_index("col")
    x, core = lax.rem(row, 4), lax.rem(col, 2)
    group = (lax.rem(lax.div(col, 2), 2) * 2 + lax.div(row, 4)) * 4 + lax.div(col, 4)
    pos = x * 2 + core

    def own_dev(k, sign):
        dx, dc = OWN[k]
        return place(group, lax.rem(x + (dx if sign > 0 else 4 - dx), 4), lax.rem(core + dc, 2))

    def partner_dev(j):
        dx, dc = PARTNER[j]
        return place(lax.rem(group + 8 - pos, GROUPS), lax.rem(x + dx, 4), lax.rem(core + dc, 2))

    def consumer_dev(j):
        dx, dc = PARTNER[j]
        cx, cc = lax.rem(x + 4 - dx, 4), lax.rem(core + dc, 2)
        return place(lax.rem(group + GROUPS - 8 + cx * 2 + cc, GROUPS), cx, cc)

    def label_dev(m, sign):
        return place(lax.rem(group + (m if sign > 0 else GROUPS - m), GROUPS), x, core)

    barrier = pltpu.get_barrier_semaphore()
    greeted = [own_dev(k, 1) for k in range(1, 8)]
    greeted += [partner_dev(j) for j in range(8)] + [consumer_dev(j) for j in range(8)]
    greeted += [label_dev(m, 1) for m in range(1, GROUPS)]
    for dev in greeted:
        pl.semaphore_signal(barrier, inc=1, device_id=dev, device_id_type=MESH)

    special = 1 - lax.div(pos + 7, 8)
    low = special * (1 - lax.div(group, 8))
    row_id = lax.broadcasted_iota(jnp.int32, (16, W), 0)

    p = points[...].astype(f32)
    half = -0.5 * jnp.sum(p * p, axis=0, keepdims=True)
    hi = half.astype(bf16).astype(f32)
    mid = (half - hi).astype(bf16).astype(f32)
    lo = half - hi - mid
    extra = jnp.where(row_id == 0, hi, jnp.where(row_id == 1, mid, jnp.where(row_id == 2, lo, 1.0)))
    blk[0, 0:F, :] = points[...]
    blk[0, F:DEPTH, :] = jnp.where(row_id < 6, extra, 0.0).astype(bf16)
    blk[0, DEPTH:ROWS, :] = direction[...].astype(bf16)
    acc[...] = jnp.zeros_like(acc)

    pl.semaphore_wait(barrier, len(greeted))

    def gather(slot, dev):
        return pltpu.make_async_remote_copy(
            src_ref=blk.at[0], dst_ref=blk.at[slot], send_sem=g_send.at[slot], recv_sem=g_recv.at[slot],
            device_id=dev, device_id_type=MESH)

    for slot in (8, 1, 2, 3, 9, 10, 11, 12, 13, 14, 15, 4, 5, 6, 7):
        gather(slot, own_dev(slot, -1) if slot < 8 else consumer_dev(slot - 8)).start()

    def arrive(slot):
        gather(slot, own_dev(1, 1)).wait_recv()

    def prepare(k):
        tail = pltpu.roll(blk[k, F:DEPTH, :].astype(f32), 3, 0)
        tail = jnp.where(row_id < 3, 1.0, jnp.where(row_id < 6, tail, 0.0)).astype(bf16)
        lhs[k] = jnp.concatenate([blk[k, 0:F, :], tail], axis=0).T

    def make(i, r, half_at):
        s = jnp.dot(lhs[i], blk[r, 0:DEPTH, :], preferred_element_type=f32)
        kbuf[half_at] = jnp.exp2(s * (math.log2(math.e) / 16.0)).astype(bf16)

    def use_rows(i, r, half_at):
        acc[i] += lax.dot_general(blk[r, DEPTH:ROWS, :], kbuf[half_at], (((1,), (1,)), ((), ())),
                                  preferred_element_type=f32)

    def use_columns(i, r, half_at):
        acc[r] += jnp.dot(blk[i, DEPTH:ROWS, :], kbuf[half_at], preferred_element_type=f32)

    prepare(0)
    make(0, 0, 0)
    use_columns(0, 0, 0)

    def tile(b, u):
        second, bb = lax.div(b, 8), lax.rem(b, 8)
        i_a = low * 4 * lax.div(bb, 4) + u
        r_a = 8 + (1 - low) * bb + low * (2 + lax.rem(bb, 4))
        i_s = 4 * lax.rem(bb, 2) + u
        r_s = lax.rem(i_s + 1 + lax.div(bb, 2), 8)
        i = (1 - second) * i_a + second * ((1 - special) * (4 + u) + special * i_s)
        r = (1 - second) * r_a + second * ((1 - special) * (8 + bb) + special * r_s)
        return i, r

    def give(slot, dev):
        return pltpu.make_async_remote_copy(
            src_ref=acc.at[slot], dst_ref=rs.at[slot], send_sem=r_send.at[slot], recv_sem=r_recv.at[slot],
            device_id=dev, device_id_type=MESH)

    for k in range(1, 4):
        arrive(k)
        prepare(k)
    arrive(8)

    @pl.when(low == 1)
    def _():
        arrive(9)
        arrive(10)

    make(*tile(0, 0), 0)

    def body(b, carry):
        ahead = b + 1 + 2 * low

        @pl.when(ahead < 8)
        def _():
            arrive(8 + ahead)

        @pl.when(b == 7 - 4 * low)
        def _():
            for k in range(4, 8):
                arrive(k)
                prepare(k)

        for j in range(6):
            @pl.when(b == 9 + j)
            def _():
                give(8 + j, partner_dev(j)).start()

        @pl.when(b == 15)
        def _():
            give(14, partner_dev(6)).start()

        @pl.when(b + 100 * special == 8)
        def _():
            for k in range(1, 4):
                give(k, own_dev(k, 1)).start()

        after = b + 1 - lax.div(b + 1, 16)
        for u in range(4):
            make(*(tile(b, u + 1) if u < 3 else tile(after, 0)), (u + 1) % 2)
            i, r = tile(b, u)
            use_rows(i, r, u % 2)
            use_columns(i, r, u % 2)
        return carry

    lax.fori_loop(0, 16 - special, body, 0)

    give(15, partner_dev(7)).start()

    @pl.when(special == 1)
    def _():
        give(14, partner_dev(6)).start()
        for k in range(1, 4):
            give(k, own_dev(k, 1)).start()

    for k in (6, 7, 4, 5):
        give(k, own_dev(k, 1)).start()

    total = direction[...] + acc[0]
    for slot in (8, 9, 10, 11, 12, 13, 14, 1, 2, 3, 15, 4, 5, 6, 7):
        give(slot, own_dev(1, 1)).wait_recv()
        total += rs[slot]
    image[...] = total

    res, dirn = residual[...], direction[...]
    sums = [jnp.sum(v, axis=1, keepdims=True) for v in (res * res, dirn * total, res * total, total * total)]
    lane = lax.broadcasted_iota(jnp.int32, (8, 128), 1)
    packed = jnp.zeros((8, 128), f32)
    for n, v in enumerate(sums):
        packed = jnp.where(lane == n, v[0:8], jnp.where(lane == n + 4, v[8:16], packed))
    stat[0] = packed

    def share(src, dst, send, recv, m, dev):
        return pltpu.make_async_remote_copy(
            src_ref=stat.at[src], dst_ref=dst.at[m], send_sem=send.at[m], recv_sem=recv.at[m],
            device_id=dev, device_id_type=MESH)

    for k in range(1, 8):
        share(0, st1, a_send, a_recv, k, own_dev(k, -1)).start()
    for k in range(1, 8):
        share(0, st1, a_send, a_recv, k, own_dev(1, 1)).wait_recv()
        packed += st1[k]
    stat[1] = packed
    for m in range(1, GROUPS):
        share(1, st2, b_send, b_recv, m, label_dev(m, 1)).start()
    for m in range(1, GROUPS):
        share(1, st2, b_send, b_recv, m, own_dev(1, 1)).wait_recv()
        packed += st2[m]

    def pick(n):
        top = jnp.sum(jnp.where(lane == n, packed, 0.0), axis=1, keepdims=True)
        bottom = jnp.sum(jnp.where(lane == n + 4, packed, 0.0), axis=1, keepdims=True)
        return jnp.broadcast_to(jnp.concatenate([top, bottom], axis=0), (R, W))

    old, curvature, cross, square = (pick(n) for n in range(4))
    step = old / curvature
    new = old + step * (step * square - 2.0 * cross)
    coefs[0] = step
    coefs[1] = new / old

    for slot in range(1, 16):
        gather(slot, own_dev(1, 1)).wait_send()
        give(slot, own_dev(1, 1)).wait_send()
    for k in range(1, 8):
        share(0, st1, a_send, a_recv, k, own_dev(1, 1)).wait_send()
    for m in range(1, GROUPS):
        share(1, st2, b_send, b_recv, m, own_dev(1, 1)).wait_send()


def on_device(points, solution, residual, direction):
    vmem = pl.BlockSpec(memory_space=pltpu.VMEM)
    dma = pltpu.SemaphoreType.DMA
    image, coefs = pl.pallas_call(
        step_kernel,
        out_shape=(jax.ShapeDtypeStruct((R, W), f32), jax.ShapeDtypeStruct((2, R, W), f32)),
        in_specs=[vmem] * 3,
        out_specs=(vmem, vmem),
        scratch_shapes=[
            pltpu.VMEM((16, ROWS, W), bf16),
            pltpu.VMEM((8, W, DEPTH), bf16),
            pltpu.VMEM((16, R, W), f32),
            pltpu.VMEM((2, W, W), bf16),
            pltpu.VMEM((16, R, W), f32),
            pltpu.VMEM((2, 8, 128), f32),
            pltpu.VMEM((8, 8, 128), f32),
            pltpu.VMEM((GROUPS, 8, 128), f32),
            dma((16,)), dma((16,)), dma((16,)), dma((16,)),
            dma((8,)), dma((8,)), dma((GROUPS,)), dma((GROUPS,)),
        ],
        compiler_params=pltpu.CompilerParams(
            collective_id=0, has_side_effects=True, vmem_limit_bytes=48 << 20),
        name="cg_step",
    )(points, residual, direction)
    step, beta = coefs[0], coefs[1]
    residual_next = residual - step * image
    return (solution + step * direction, residual_next, residual_next + beta * direction)


def solution(mesh):
    placed = (P(None, ("row", "col")),) * 4
    return jax.shard_map(on_device, mesh=mesh, in_specs=placed, out_specs=placed[:3], check_vma=False)
```

```python
import math

import jax
import jax.numpy as jnp
from jax import lax
from jax.experimental import pallas as pl
from jax.experimental.pallas import tpu as pltpu
from jax.sharding import PartitionSpec as P

OFFSETS = ((0, 0), (0, 1), (1, 0), (1, 1), (3, 0), (3, 1), (2, 0), (2, 1))
F, R, W = 64, 16, 512
DEPTH = F + 16
ROWS = DEPTH + R
GROUPS = 16
MESH = pl.DeviceIdType.MESH
bf16, f32 = jnp.bfloat16, jnp.float32


def step_kernel(points_hbm, residual_hbm, direction_hbm, image, coefs, points, residual, direction,
                blk, lhs, acc, kbuf, rs, stat, st1, st2,
                in_sem, g_send, g_recv, r_send, r_recv, a_send, a_recv, b_send, b_recv):
    loads = [pltpu.make_async_copy(src, dst, in_sem.at[n]) for n, (src, dst) in enumerate(
        ((points_hbm, points), (direction_hbm, direction), (residual_hbm, residual)))]
    for load in loads:
        load.start()

    row, col = lax.axis_index("row"), lax.axis_index("col")
    x, core = lax.rem(row, 4), lax.rem(col, 2)
    y, z = lax.rem(lax.div(col, 2), 2) * 2 + lax.div(row, 4), lax.div(col, 4)
    group, pos = y * 4 + z, x * 2 + core

    def beside(dev, k, sign=1):
        dx, dc = OFFSETS[k]
        there = lax.rem(x + (dx if sign > 0 else 4 - dx), 4) - x if dx else 0
        return (dev[0] + there, dev[1] + (dc * (1 - 2 * core) if dc else 0))

    def of_group(label):
        gy, gz = lax.div(label, 4), lax.rem(label, 4)
        return (lax.rem(gy, 2) * 4 + x, gz * 4 + lax.div(gy, 2) * 2 + core)

    me = (row, col)
    partner = of_group(lax.rem(group + 8 - pos, GROUPS))
    consumer = of_group(lax.rem(group + 8 + pos, GROUPS))

    barrier = pltpu.get_barrier_semaphore()
    greeted = [beside(me, k) for k in (1, 2, 4, 6)] + [partner, consumer]
    for dev in greeted:
        pl.semaphore_signal(barrier, inc=1, device_id=dev, device_id_type=MESH)

    special = 1 - lax.div(pos + 7, 8)
    upper = special * lax.div(group, 8)
    row_id = lax.broadcasted_iota(jnp.int32, (16, W), 0)

    loads[0].wait()
    p = points[...].astype(f32)
    half = -0.5 * jnp.sum(p * p, axis=0, keepdims=True)
    hi = half.astype(bf16).astype(f32)
    mid = (half - hi).astype(bf16).astype(f32)
    lo = half - hi - mid
    extra = jnp.where(row_id == 0, hi, jnp.where(row_id == 1, mid, jnp.where(row_id == 2, lo, 1.0)))
    blk[0, 0:F, :] = points[...]
    blk[0, F:DEPTH, :] = jnp.where(row_id < 6, extra, 0.0).astype(bf16)
    loads[1].wait()
    blk[0, DEPTH:ROWS, :] = direction[...].astype(bf16)
    loads[2].wait()
    acc[...] = jnp.zeros_like(acc)

    pl.semaphore_wait(barrier, len(greeted))

    def pass_on(src, dst, dev):
        return pltpu.make_async_remote_copy(
            src_ref=blk.at[src], dst_ref=blk.at[dst], send_sem=g_send.at[dst], recv_sem=g_recv.at[dst],
            device_id=dev, device_id_type=MESH)

    pass_on(0, 1, beside(me, 1)).start()
    for k in (2, 4):
        pass_on(0, k, beside(me, k, -1)).start()
    pass_on(0, 8, consumer).start()
    pass_on(0, 6, beside(me, 6)).start()

    def arrive(slot):
        pass_on(0, slot, consumer).wait_recv()

    def prepare(k):
        tail = pltpu.roll(blk[k, F:DEPTH, :].astype(f32), 3, 0)
        tail = jnp.where(row_id < 3, 1.0, jnp.where(row_id < 6, tail, 0.0)).astype(bf16)
        lhs[k] = jnp.concatenate([blk[k, 0:F, :], tail], axis=0).T

    def make(i, r, half_at):
        s = jnp.dot(lhs[i], blk[r, 0:DEPTH, :], preferred_element_type=f32)
        kbuf[half_at] = jnp.exp2(s * (math.log2(math.e) / 16.0)).astype(bf16)

    def use_rows(i, r, half_at):
        acc[i] += lax.dot_general(blk[r, DEPTH:ROWS, :], kbuf[half_at], (((1,), (1,)), ((), ())),
                                  preferred_element_type=f32)

    def use_columns(i, r, half_at):
        acc[r] += jnp.dot(blk[i, DEPTH:ROWS, :], kbuf[half_at], preferred_element_type=f32)

    def own_block(k):
        arrive(k)
        if k in (2, 4, 6):
            pass_on(k, k + 1, beside(me, 1)).start()
        pass_on(k, 8 + k, consumer).start()
        prepare(k)

    prepare(0)
    make(0, 0, 0)
    use_columns(0, 0, 0)

    def tile(b, u):
        second, bb = lax.div(b, 8), lax.rem(b, 8)
        quarter, j4 = lax.div(bb, 4), lax.rem(bb, 4)
        i_a = 4 * (upper + (1 - upper) * quarter) + u
        r_a = 8 + j4 + 4 * upper * quarter
        i_n = 4 * (1 - quarter) + u
        r_n = 12 + j4
        i_s = 4 * lax.rem(bb, 2) + u
        r_s = lax.rem(i_s + 1 + lax.div(bb, 2), 8)
        i = (1 - second) * i_a + second * ((1 - special) * i_n + special * i_s)
        r = (1 - second) * r_a + second * ((1 - special) * r_n + special * r_s)
        return i, r

    def give(slot, dev):
        return pltpu.make_async_remote_copy(
            src_ref=acc.at[slot], dst_ref=rs.at[slot], send_sem=r_send.at[slot], recv_sem=r_recv.at[slot],
            device_id=dev, device_id_type=MESH)

    def give_partner(j):
        give(8 + j, beside(partner, j)).start()

    def give_own(k):
        give(k, beside(me, k)).start()

    for k in (1, 2, 4, 3):
        own_block(k)

    @pl.when(upper == 1)
    def _():
        for k in (5, 6, 7):
            own_block(k)

    arrive(8)
    make(*tile(0, 0), 0)

    def body(b, carry):
        for k in (5, 6, 7):
            @pl.when(b + 100 * upper == k - 5)
            def _():
                own_block(k)

        early = jnp.logical_and(b < 7, jnp.logical_or(b < 3, upper == 1))
        late = jnp.logical_and(jnp.logical_and(b >= 7, b < 11), upper == 0)

        @pl.when(early)
        def _():
            arrive(9 + b)

        @pl.when(late)
        def _():
            arrive(5 + b)

        for j in range(7):
            @pl.when(b == (6 + j if j < 4 else 9 + j))
            def _():
                give_partner(j)

        @pl.when(b + 100 * special == 12)
        def _():
            for k in (6, 7, 4, 5):
                give_own(k)

        after = b + 1 - lax.div(b + 1, 16)
        for u in range(4):
            make(*(tile(b, u + 1) if u < 3 else tile(after, 0)), (u + 1) % 2)
            i, r = tile(b, u)
            use_rows(i, r, u % 2)
            use_columns(i, r, u % 2)
        return carry

    lax.fori_loop(0, 16 - special, body, 0)

    @pl.when(special == 1)
    def _():
        for k in (6, 7, 4, 5):
            give_own(k)
        give_partner(6)

    give_partner(7)
    for k in (2, 3, 1):
        give_own(k)

    total = direction[...] + acc[0]
    for slot in (8, 9, 10, 11, 12, 13, 6, 7, 4, 5, 14, 15, 1, 2, 3):
        give(slot, me).wait_recv()
        total += rs[slot]
    image[...] = total

    res, dirn = residual[...], direction[...]
    sums = [jnp.sum(v, axis=1, keepdims=True) for v in (res * res, dirn * total, res * total, total * total)]
    lane = lax.broadcasted_iota(jnp.int32, (8, 128), 1)
    packed = jnp.zeros((8, 128), f32)
    for n, v in enumerate(sums):
        packed = jnp.where(lane == n, v[0:8], jnp.where(lane == n + 4, v[8:16], packed))
    stat[0] = packed

    def share(src, dst, send, recv, m, dev):
        return pltpu.make_async_remote_copy(
            src_ref=stat.at[src], dst_ref=dst.at[m], send_sem=send.at[m], recv_sem=recv.at[m],
            device_id=dev, device_id_type=MESH)

    for k in (6, 7, 2, 3, 4, 5, 1):
        share(0, st1, a_send, a_recv, k, beside(me, k, -1)).start()
    ys = [lax.rem(y + d, 4) for d in range(4)]
    zs = [lax.rem(z + d, 4) * 4 for d in range(4)]
    rows = [lax.rem(v, 2) * 4 + x for v in ys]
    cols = [lax.div(v, 2) * 2 + core for v in ys]
    for k in (1, 2, 3, 4, 5, 6, 7):
        share(0, st1, a_send, a_recv, k, me).wait_recv()
        packed += st1[k]
    stat[1] = packed
    order = (10, 6, 14, 9, 11, 2, 8, 5, 7, 13, 15, 1, 3, 4, 12)
    for m in order:
        share(1, st2, b_send, b_recv, m, (rows[m // 4], cols[m // 4] + zs[m % 4])).start()
    for m in reversed(order):
        share(1, st2, b_send, b_recv, m, me).wait_recv()
        packed += st2[m]

    def pick(n):
        top = jnp.sum(jnp.where(lane == n, packed, 0.0), axis=1, keepdims=True)
        bottom = jnp.sum(jnp.where(lane == n + 4, packed, 0.0), axis=1, keepdims=True)
        return jnp.broadcast_to(jnp.concatenate([top, bottom], axis=0), (R, W))

    old, curvature, cross, square = (pick(n) for n in range(4))
    step = old / curvature
    new = old + step * (step * square - 2.0 * cross)
    coefs[0] = step
    coefs[1] = new / old

    for slot in range(1, 16):
        pass_on(0, slot, consumer).wait_send()
        give(slot, me).wait_send()
    for k in range(1, 8):
        share(0, st1, a_send, a_recv, k, me).wait_send()
    for m in range(1, GROUPS):
        share(1, st2, b_send, b_recv, m, me).wait_send()


def on_device(points, solution, residual, direction):
    vmem = pl.BlockSpec(memory_space=pltpu.VMEM)
    dma = pltpu.SemaphoreType.DMA
    image, coefs = pl.pallas_call(
        step_kernel,
        out_shape=(jax.ShapeDtypeStruct((R, W), f32), jax.ShapeDtypeStruct((2, R, W), f32)),
        in_specs=[pl.BlockSpec(memory_space=pltpu.HBM)] * 3,
        out_specs=(vmem, vmem),
        scratch_shapes=[
            pltpu.VMEM((F, W), bf16),
            pltpu.VMEM((R, W), f32),
            pltpu.VMEM((R, W), f32),
            pltpu.VMEM((16, ROWS, W), bf16),
            pltpu.VMEM((8, W, DEPTH), bf16),
            pltpu.VMEM((16, R, W), f32),
            pltpu.VMEM((2, W, W), bf16),
            pltpu.VMEM((16, R, W), f32),
            pltpu.VMEM((2, 8, 128), f32),
            pltpu.VMEM((8, 8, 128), f32),
            pltpu.VMEM((GROUPS, 8, 128), f32),
            dma((3,)), dma((16,)), dma((16,)), dma((16,)), dma((16,)),
            dma((8,)), dma((8,)), dma((GROUPS,)), dma((GROUPS,)),
        ],
        compiler_params=pltpu.CompilerParams(
            collective_id=0, has_side_effects=True, vmem_limit_bytes=48 << 20),
        name="cg_step",
    )(points, residual, direction)
    step, beta = coefs[0], coefs[1]
    residual_next = residual - step * image
    return (solution + step * direction, residual_next, residual_next + beta * direction)


def solution(mesh):
    placed = (P(None, ("row", "col")),) * 4
    return jax.shard_map(on_device, mesh=mesh, in_specs=placed, out_specs=placed[:3], check_vma=False)
```

```python
import math

import jax
import jax.numpy as jnp
from jax import lax
from jax.experimental import pallas as pl
from jax.experimental.pallas import tpu as pltpu
from jax.sharding import PartitionSpec as P

OFFSETS = ((0, 0), (0, 1), (1, 0), (3, 0), (2, 0), (2, 1), (1, 1), (3, 1))
SIBLING = 1
RELAYED = {2: 6, 3: 7, 4: 5}
SHIFT = ((2, 2), (1, 1), (1, 2), (3, 0), (2, 1), (0, 3), (0, 0), (1, 3))
F, R, W = 64, 16, 512
DEPTH = F + 16
ROWS = DEPTH + R
GROUPS = 16
MESH = pl.DeviceIdType.MESH
bf16, f32 = jnp.bfloat16, jnp.float32


def step_kernel(points_hbm, residual_hbm, direction_hbm, image, coefs, points, residual, direction,
                blk, lhs, acc, kbuf, rs, stat, st1, st2,
                in_sem, g_send, g_recv, r_send, r_recv, a_send, a_recv, b_send, b_recv):
    loads = [pltpu.make_async_copy(src, dst, in_sem.at[n]) for n, (src, dst) in enumerate(
        ((points_hbm, points), (direction_hbm, direction), (residual_hbm, residual)))]
    for load in loads:
        load.start()

    row, col = lax.axis_index("row"), lax.axis_index("col")
    x, core = lax.rem(row, 4), lax.rem(col, 2)
    y, z = lax.rem(lax.div(col, 2), 2) * 2 + lax.div(row, 4), lax.div(col, 4)
    pos = x * 2 + core

    def beside(dev, k, sign=1):
        dx, dc = OFFSETS[k]
        there = lax.rem(x + (dx if sign > 0 else 4 - dx), 4) - x if dx else 0
        return (dev[0] + there, dev[1] + (dc * (1 - 2 * core) if dc else 0))

    def choose(values):
        return sum(jnp.where(pos == n, v, 0) for n, v in enumerate(values) if v)

    def moved(dy, dz):
        gy, gz = lax.rem(y + dy, 4), lax.rem(z + dz, 4)
        return (lax.rem(gy, 2) * 4 + x, gz * 4 + lax.div(gy, 2) * 2 + core)

    me = (row, col)
    turn = lax.rem(lax.div(y, 2) + lax.div(z, 2), 2)
    square = choose((0,) * 6 + (2, 0))
    shift_y, shift_z = choose([v[0] for v in SHIFT]), choose([v[1] for v in SHIFT])
    partner = moved(shift_y + square * (1 - turn), shift_z + square * turn)
    consumer = moved(4 - shift_y - square * turn, 4 - shift_z - square * (1 - turn))

    barrier = pltpu.get_barrier_semaphore()
    greeted = [beside(me, k) for k in (SIBLING, 2, 3, 4)] + [partner, consumer]
    for dev in greeted:
        pl.semaphore_signal(barrier, inc=1, device_id=dev, device_id_type=MESH)

    special = 1 - lax.div(pos + 7, 8)
    upper = special * lax.div(y, 2)
    normal = 1 - special
    row_id = lax.broadcasted_iota(jnp.int32, (16, W), 0)

    loads[0].wait()
    p = points[...].astype(f32)
    half = -0.5 * jnp.sum(p * p, axis=0, keepdims=True)
    hi = half.astype(bf16).astype(f32)
    mid = (half - hi).astype(bf16).astype(f32)
    lo = half - hi - mid
    extra = jnp.where(row_id == 0, hi, jnp.where(row_id == 1, mid, jnp.where(row_id == 2, lo, 1.0)))
    blk[0, 0:F, :] = points[...]
    blk[0, F:DEPTH, :] = jnp.where(row_id < 6, extra, 0.0).astype(bf16)
    loads[1].wait()
    blk[0, DEPTH:ROWS, :] = direction[...].astype(bf16)
    loads[2].wait()
    acc[...] = jnp.zeros_like(acc)

    pl.semaphore_wait(barrier, len(greeted))

    def pass_on(src, dst, dev):
        return pltpu.make_async_remote_copy(
            src_ref=blk.at[src], dst_ref=blk.at[dst], send_sem=g_send.at[dst], recv_sem=g_recv.at[dst],
            device_id=dev, device_id_type=MESH)

    for k in (2, 3):
        pass_on(0, k, beside(me, k, -1)).start()
    pass_on(0, 8, consumer).start()
    pass_on(0, SIBLING, beside(me, SIBLING)).start()
    pass_on(0, 4, beside(me, 4)).start()

    def arrive(slot):
        pass_on(0, slot, consumer).wait_recv()

    def prepare(k):
        tail = pltpu.roll(blk[k, F:DEPTH, :].astype(f32), 3, 0)
        tail = jnp.where(row_id < 3, 1.0, jnp.where(row_id < 6, tail, 0.0)).astype(bf16)
        lhs[k] = jnp.concatenate([blk[k, 0:F, :], tail], axis=0).T

    def make(i, r, half_at):
        s = jnp.dot(lhs[i], blk[r, 0:DEPTH, :], preferred_element_type=f32)
        kbuf[half_at] = jnp.exp2(s * (math.log2(math.e) / 16.0)).astype(bf16)

    def use_rows(i, r, half_at):
        acc[i] += lax.dot_general(blk[r, DEPTH:ROWS, :], kbuf[half_at], (((1,), (1,)), ((), ())),
                                  preferred_element_type=f32)

    def use_columns(i, r, half_at):
        acc[r] += jnp.dot(blk[i, DEPTH:ROWS, :], kbuf[half_at], preferred_element_type=f32)

    def own_block(k):
        arrive(k)
        if k in RELAYED:
            pass_on(k, RELAYED[k], beside(me, SIBLING)).start()

    def forward(k):
        pass_on(k, 8 + k, consumer).start()

    prepare(0)
    make(0, 0, 0)
    use_columns(0, 0, 0)

    def tile(b, u):
        half, parity = lax.div(b, 2), lax.rem(b, 2)
        swap = special * (lax.div(b + 3, 16) - lax.div(b + 1, 16))
        half_s = half + swap * parity
        parity_s = parity + swap * (1 - 2 * parity)
        half_s = half_s - swap * (1 - parity)
        first, start = 1 - lax.div(b + 14, 16), 1 - lax.div(b + 12, 16)
        cross = start - first
        i_n = (1 - start) * 4 * (1 - parity) + cross * (6 - 2 * parity) + (1 - cross) * u + cross * (u % 2)
        j_n = first * parity + cross * (u // 2) + (1 - start) * half
        hh, pair = lax.rem(half_s, 2), lax.div(half_s, 2)
        i_p = 4 * hh + upper * 2 * (u % 2) + (1 - upper) * u
        j_p = 2 * pair + upper * (u // 2) + (1 - upper)
        i_s = 4 * hh + u
        r_s = lax.rem(i_s + 1 + pair, 8)
        i = normal * i_n + special * ((1 - parity_s) * i_p + parity_s * i_s)
        r = normal * (8 + j_n) + special * ((1 - parity_s) * (8 + j_p) + parity_s * r_s)
        return i, r

    def give(slot, dev):
        return pltpu.make_async_remote_copy(
            src_ref=acc.at[slot], dst_ref=rs.at[slot], send_sem=r_send.at[slot], recv_sem=r_recv.at[slot],
            device_id=dev, device_id_type=MESH)

    def give_partner(j):
        give(8 + j, beside(partner, j)).start()

    def give_own(k):
        give(k, beside(me, k)).start()

    own_block(1)
    forward(1)
    prepare(1)
    for k in (2, 3):
        own_block(k)
    for k in (2, 3):
        forward(k)
        prepare(k)
    arrive(8)

    @pl.when(special == 1)
    def _():
        arrive(9)

    def work(b, b_next, us):
        for u in us:
            make(*(tile(b, u + 1) if u < 3 else tile(b_next, 0)), (u + 1) % 2)
            i, r = tile(b, u)
            use_rows(i, r, u % 2)
            use_columns(i, r, u % 2)

    make(*tile(0, 0), 0)
    work(0, 0, range(3))

    @pl.when(special == 0)
    def _():
        arrive(9)

    work(0, 1, (3,))

    def body(b, carry):
        @pl.when(b == 1)
        def _():
            for k in (6, 7):
                own_block(k)
                prepare(k)

        @pl.when(b == 2 - special)
        def _():
            own_block(4)
            forward(4)
            prepare(4)

        @pl.when(b == 3 - special)
        def _():
            own_block(5)
            prepare(5)
            for k in (5, 6, 7):
                forward(k)

        for j in range(2, 8):
            @pl.when(b == normal * (2 * j - 1) + special * (4 * (j // 2) - 1))
            def _():
                arrive(8 + j)

        for j in range(7):
            @pl.when(b == (2 * j + 3 if j else 4))
            def _():
                give_partner(j)

        @pl.when(b == 14 + 100 * (1 - special))
        def _():
            give_partner(6)
            give_partner(7)

        @pl.when(b + 100 * special == 15)
        def _():
            for k in (4, 5, 6, 7):
                give_own(k)

        work(b, b + 1 - lax.div(b + 1, 16), range(4))
        return carry

    lax.fori_loop(1, 16 - special, body, 0)

    @pl.when(special == 1)
    def _():
        for k in (4, 5, 6, 7):
            give_own(k)

    @pl.when(special == 0)
    def _():
        give_partner(7)

    for k in (2, 3, 1):
        give_own(k)

    total = direction[...] + acc[0]
    for slot in (8, 9, 10, 11, 12, 13, 14, 6, 7, 4, 5, 1, 2, 3, 15):
        give(slot, me).wait_recv()
        total += rs[slot]
    image[...] = total

    res, dirn = residual[...], direction[...]
    sums = [jnp.sum(v, axis=1, keepdims=True) for v in (res * res, dirn * total, res * total, total * total)]
    lane = lax.broadcasted_iota(jnp.int32, (8, 128), 1)
    packed = jnp.zeros((8, 128), f32)
    for n, v in enumerate(sums):
        packed = jnp.where(lane == n, v[0:8], jnp.where(lane == n + 4, v[8:16], packed))
    stat[0] = packed

    def share(src, dst, send, recv, m, dev):
        return pltpu.make_async_remote_copy(
            src_ref=stat.at[src], dst_ref=dst.at[m], send_sem=send.at[m], recv_sem=recv.at[m],
            device_id=dev, device_id_type=MESH)

    for k in (4, 5, 2, 3, 6, 7, 1):
        share(0, st1, a_send, a_recv, k, beside(me, k, -1)).start()
    ys = [lax.rem(y + d, 4) for d in range(4)]
    zs = [lax.rem(z + d, 4) * 4 for d in range(4)]
    rows = [lax.rem(v, 2) * 4 + x for v in ys]
    cols = [lax.div(v, 2) * 2 + core for v in ys]
    for k in (1, 2, 3, 6, 7, 4, 5):
        share(0, st1, a_send, a_recv, k, me).wait_recv()
        packed += st1[k]
    stat[1] = packed
    order = (10, 6, 14, 9, 11, 2, 8, 5, 7, 13, 15, 1, 3, 4, 12)
    for m in order:
        share(1, st2, b_send, b_recv, m, (rows[m // 4], cols[m // 4] + zs[m % 4])).start()
    for m in reversed(order):
        share(1, st2, b_send, b_recv, m, me).wait_recv()
        packed += st2[m]

    def pick(n):
        top = jnp.sum(jnp.where(lane == n, packed, 0.0), axis=1, keepdims=True)
        bottom = jnp.sum(jnp.where(lane == n + 4, packed, 0.0), axis=1, keepdims=True)
        return jnp.broadcast_to(jnp.concatenate([top, bottom], axis=0), (R, W))

    old, curvature, cross, square = (pick(n) for n in range(4))
    step = old / curvature
    new = old + step * (step * square - 2.0 * cross)
    coefs[0] = step
    coefs[1] = new / old

    for slot in range(1, 16):
        pass_on(0, slot, consumer).wait_send()
        give(slot, me).wait_send()
    for k in range(1, 8):
        share(0, st1, a_send, a_recv, k, me).wait_send()
    for m in range(1, GROUPS):
        share(1, st2, b_send, b_recv, m, me).wait_send()


def on_device(points, solution, residual, direction):
    vmem = pl.BlockSpec(memory_space=pltpu.VMEM)
    dma = pltpu.SemaphoreType.DMA
    image, coefs = pl.pallas_call(
        step_kernel,
        out_shape=(jax.ShapeDtypeStruct((R, W), f32), jax.ShapeDtypeStruct((2, R, W), f32)),
        in_specs=[pl.BlockSpec(memory_space=pltpu.HBM)] * 3,
        out_specs=(vmem, vmem),
        scratch_shapes=[
            pltpu.VMEM((F, W), bf16),
            pltpu.VMEM((R, W), f32),
            pltpu.VMEM((R, W), f32),
            pltpu.VMEM((16, ROWS, W), bf16),
            pltpu.VMEM((8, W, DEPTH), bf16),
            pltpu.VMEM((16, R, W), f32),
            pltpu.VMEM((2, W, W), bf16),
            pltpu.VMEM((16, R, W), f32),
            pltpu.VMEM((2, 8, 128), f32),
            pltpu.VMEM((8, 8, 128), f32),
            pltpu.VMEM((GROUPS, 8, 128), f32),
            dma((3,)), dma((16,)), dma((16,)), dma((16,)), dma((16,)),
            dma((8,)), dma((8,)), dma((GROUPS,)), dma((GROUPS,)),
        ],
        compiler_params=pltpu.CompilerParams(
            collective_id=0, has_side_effects=True, vmem_limit_bytes=67000000),
        name="cg_step",
    )(points, residual, direction)
    step, beta = coefs[0], coefs[1]
    residual_next = residual - step * image
    return (solution + step * direction, residual_next, residual_next + beta * direction)


def solution(mesh):
    placed = (P(None, ("row", "col")),) * 4
    return jax.shard_map(on_device, mesh=mesh, in_specs=placed, out_specs=placed[:3], check_vma=False)
```

```python
import math

import jax
import jax.numpy as jnp
from jax import lax
from jax.experimental import pallas as pl
from jax.experimental.pallas import tpu as pltpu
from jax.sharding import PartitionSpec as P

OFFSETS = ((0, 0), (0, 1), (1, 0), (3, 0), (2, 0), (2, 1), (1, 1), (3, 1))
SIBLING = 1
RELAYED = {2: 6, 3: 7, 4: 5}
SHIFT = ((2, 2), (1, 1), (1, 2), (3, 0), (2, 1), (0, 3), (0, 0), (1, 3))
F, R, W = 64, 16, 512
SENT = R + F
DEPTH = F + 16
ROWS = SENT + 16
GROUPS = 16
MESH = pl.DeviceIdType.MESH
bf16, f32 = jnp.bfloat16, jnp.float32


def step_kernel(points_hbm, residual_hbm, direction_hbm, image, coefs, points, residual, direction,
                blk, lhs, acc, kbuf, rs, stat, st1, st2,
                in_sem, g_send, g_recv, r_send, r_recv, a_send, a_recv, b_send, b_recv):
    loads = [pltpu.make_async_copy(src, dst, in_sem.at[n]) for n, (src, dst) in enumerate(
        ((points_hbm, points), (direction_hbm, direction), (residual_hbm, residual)))]
    for load in loads:
        load.start()

    row, col = lax.axis_index("row"), lax.axis_index("col")
    x, core = lax.rem(row, 4), lax.rem(col, 2)
    y, z = lax.rem(lax.div(col, 2), 2) * 2 + lax.div(row, 4), lax.div(col, 4)
    pos = x * 2 + core

    def beside(dev, k, sign=1):
        dx, dc = OFFSETS[k]
        there = lax.rem(x + (dx if sign > 0 else 4 - dx), 4) - x if dx else 0
        return (dev[0] + there, dev[1] + (dc * (1 - 2 * core) if dc else 0))

    def choose(values):
        return sum(jnp.where(pos == n, v, 0) for n, v in enumerate(values) if v)

    def moved(dy, dz):
        gy, gz = lax.rem(y + dy, 4), lax.rem(z + dz, 4)
        return (lax.rem(gy, 2) * 4 + x, gz * 4 + lax.div(gy, 2) * 2 + core)

    me = (row, col)
    turn = lax.rem(lax.div(y, 2) + lax.div(z, 2), 2)
    square = choose((0,) * 6 + (2, 0))
    shift_y, shift_z = choose([v[0] for v in SHIFT]), choose([v[1] for v in SHIFT])
    partner = moved(shift_y + square * (1 - turn), shift_z + square * turn)
    consumer = moved(4 - shift_y - square * turn, 4 - shift_z - square * (1 - turn))

    barrier = pltpu.get_barrier_semaphore()
    greeted = [beside(me, k) for k in (SIBLING, 2, 3, 4)] + [partner, consumer]
    for dev in greeted:
        pl.semaphore_signal(barrier, inc=1, device_id=dev, device_id_type=MESH)

    special = 1 - lax.div(pos + 7, 8)
    upper = special * lax.div(y, 2)
    lower = special - upper
    normal = 1 - special
    row_id = lax.broadcasted_iota(jnp.int32, (16, W), 0)

    def extend(slot):
        p = blk[slot, R:SENT, :].astype(f32)
        half = -0.5 * jnp.sum(p * p, axis=0, keepdims=True)
        hi = half.astype(bf16).astype(f32)
        mid = (half - hi).astype(bf16).astype(f32)
        lo = half - hi - mid
        pieces = jnp.where(row_id == 0, hi, jnp.where(row_id == 1, mid, jnp.where(row_id == 2, lo, 1.0)))
        blk[slot, SENT:ROWS, :] = jnp.where(row_id < 6, pieces, 0.0).astype(bf16)

    for load in loads:
        load.wait()
    blk[0, 0:R, :] = direction[...].astype(bf16)
    blk[0, R:SENT, :] = points[...]
    extend(0)
    acc[...] = jnp.zeros_like(acc)

    pl.semaphore_wait(barrier, len(greeted))

    def pass_on(src, dst, dev):
        return pltpu.make_async_remote_copy(
            src_ref=blk.at[src, pl.ds(0, SENT)], dst_ref=blk.at[dst, pl.ds(0, SENT)], send_sem=g_send.at[dst], recv_sem=g_recv.at[dst],
            device_id=dev, device_id_type=MESH)

    def forward(k):
        if k % 2:
            pass_on(k, 8 + k, consumer).start()
        else:
            @pl.when(upper == 0)
            def _():
                pass_on(k, 8 + k, consumer).start()

    forward(0)
    for k in (2, 3):
        pass_on(0, k, beside(me, k, -1)).start()
    pass_on(0, SIBLING, beside(me, SIBLING)).start()
    pass_on(0, 4, beside(me, 4)).start()

    def arrive(slot):
        pass_on(0, slot, consumer).wait_recv()
        extend(slot)

    def prepare(k):
        tail = pltpu.roll(blk[k, SENT:ROWS, :].astype(f32), 3, 0)
        tail = jnp.where(row_id < 3, 1.0, jnp.where(row_id < 6, tail, 0.0)).astype(bf16)
        lhs[k] = jnp.concatenate([blk[k, R:SENT, :], tail], axis=0).T

    def make(i, r, half_at):
        s = jnp.dot(lhs[i], blk[r, R:ROWS, :], preferred_element_type=f32)
        kbuf[half_at] = jnp.exp2(s * (math.log2(math.e) / 16.0)).astype(bf16)

    def use_rows(i, r, half_at):
        acc[i] += lax.dot_general(blk[r, 0:R, :], kbuf[half_at], (((1,), (1,)), ((), ())),
                                  preferred_element_type=f32)

    def use_columns(i, r, half_at):
        acc[r] += jnp.dot(blk[i, 0:R, :], kbuf[half_at], preferred_element_type=f32)

    def own_block(k):
        arrive(k)
        if k in RELAYED:
            pass_on(k, RELAYED[k], beside(me, SIBLING)).start()

    prepare(0)
    make(0, 0, 0)
    use_columns(0, 0, 0)

    def tile(b, u):
        half, parity = lax.div(b, 2), lax.rem(b, 2)
        swap = special * (lax.div(b + 3, 16) - lax.div(b + 1, 16))
        half_s = half + swap * parity
        parity_s = parity + swap * (1 - 2 * parity)
        half_s = half_s - swap * (1 - parity)
        early, zero, last = 1 - lax.div(b + 13, 16), 1 - lax.div(b + 15, 16), lax.div(b + 1, 16)
        cross = early - zero
        i_n = cross * (8 - 2 * b + u % 2) + (1 - cross) * (4 * parity * (1 - last) + u)
        j_n = cross * (u // 2) + (1 - early) * ((1 - last) * lax.div(b + 1, 2) + last)
        hh, pair = lax.rem(half_s, 2), lax.div(half_s, 2)
        i_p = 4 * hh + upper * 2 * (u % 2) + (1 - upper) * u
        j_p = 2 * pair + upper * (u // 2) + (1 - upper)
        i_s = 4 * hh + u
        r_s = lax.rem(i_s + 1 + pair, 8)
        i = normal * i_n + special * ((1 - parity_s) * i_p + parity_s * i_s)
        r = normal * (8 + j_n) + special * ((1 - parity_s) * (8 + j_p) + parity_s * r_s)
        return i, r

    def give(slot, dev):
        return pltpu.make_async_remote_copy(
            src_ref=acc.at[slot], dst_ref=rs.at[slot], send_sem=r_send.at[slot], recv_sem=r_recv.at[slot],
            device_id=dev, device_id_type=MESH)

    def give_partner(j):
        give(8 + j, beside(partner, j)).start()

    def give_own(k):
        give(k, beside(me, k)).start()

    own_block(1)
    forward(1)
    prepare(1)
    for k in (2, 3):
        own_block(k)
    for k in (2, 3):
        forward(k)
        prepare(k)

    @pl.when(lower == 0)
    def _():
        arrive(8)

    @pl.when(special == 1)
    def _():
        arrive(9)

    def work(b, b_next, us):
        for u in us:
            make(*(tile(b, u + 1) if u < 3 else tile(b_next, 0)), (u + 1) % 2)
            i, r = tile(b, u)
            use_rows(i, r, u % 2)
            use_columns(i, r, u % 2)

    make(*tile(0, 0), 0)
    work(0, 0, range(3))

    for k in (6, 7):
        own_block(k)
        prepare(k)

    work(0, 1, (3,))

    def body(b, carry):
        @pl.when(b == 1)
        def _():
            own_block(4)
            forward(4)
            prepare(4)

            @pl.when(special == 0)
            def _():
                arrive(9)

        @pl.when(b == 2)
        def _():
            own_block(5)
            prepare(5)
            for k in (5, 6, 7):
                forward(k)

        for j in range(2, 8):
            @pl.when(b == normal * (2 * j - 2) + special * (4 * (j // 2) - 1) + (0 if j % 2 else 100 * lower))
            def _():
                arrive(8 + j)

        for j, at in ((0, 4), (1, 5 + 100 * normal), (2, 7), (3, 8), (4, 11), (5, 12), (6, 14), (7, 14 + normal)):
            @pl.when(b == at)
            def _():
                give_partner(j)

        @pl.when(b + 100 * special == 14)
        def _():
            for k in (4, 5, 6, 7):
                give_own(k)

        work(b, b + 1 - lax.div(b + 1, 16), range(4))
        return carry

    lax.fori_loop(1, 16 - special, body, 0)

    @pl.when(special == 1)
    def _():
        for k in (4, 5, 6, 7):
            give_own(k)

    @pl.when(special == 0)
    def _():
        give_partner(1)

    for k in (2, 3, 1):
        give_own(k)

    total = direction[...] + acc[0]
    for slot in (8, 10, 11, 12, 13, 14, 15, 6, 7, 4, 5, 1, 2, 3, 9):
        give(slot, me).wait_recv()
        total += rs[slot]
    image[...] = total

    res, dirn = residual[...], direction[...]
    sums = [jnp.sum(v, axis=1, keepdims=True) for v in (res * res, dirn * total, res * total, total * total)]
    lane = lax.broadcasted_iota(jnp.int32, (8, 128), 1)
    packed = jnp.zeros((8, 128), f32)
    for n, v in enumerate(sums):
        packed = jnp.where(lane == n, v[0:8], jnp.where(lane == n + 4, v[8:16], packed))
    stat[0] = packed

    def share(src, dst, send, recv, m, dev):
        return pltpu.make_async_remote_copy(
            src_ref=stat.at[src], dst_ref=dst.at[m], send_sem=send.at[m], recv_sem=recv.at[m],
            device_id=dev, device_id_type=MESH)

    for k in (4, 5, 2, 3, 6, 7, 1):
        share(0, st1, a_send, a_recv, k, beside(me, k, -1)).start()
    ys = [lax.rem(y + d, 4) for d in range(4)]
    zs = [lax.rem(z + d, 4) * 4 for d in range(4)]
    rows = [lax.rem(v, 2) * 4 + x for v in ys]
    cols = [lax.div(v, 2) * 2 + core for v in ys]
    for k in (1, 2, 3, 6, 7, 4, 5):
        share(0, st1, a_send, a_recv, k, me).wait_recv()
        packed += st1[k]
    stat[1] = packed
    order = (10, 6, 14, 9, 11, 2, 8, 5, 7, 13, 15, 1, 3, 4, 12)
    for m in order:
        share(1, st2, b_send, b_recv, m, (rows[m // 4], cols[m // 4] + zs[m % 4])).start()
    for m in reversed(order):
        share(1, st2, b_send, b_recv, m, me).wait_recv()
        packed += st2[m]

    def pick(n):
        top = jnp.sum(jnp.where(lane == n, packed, 0.0), axis=1, keepdims=True)
        bottom = jnp.sum(jnp.where(lane == n + 4, packed, 0.0), axis=1, keepdims=True)
        return jnp.broadcast_to(jnp.concatenate([top, bottom], axis=0), (R, W))

    old, curvature, cross, square = (pick(n) for n in range(4))
    step = old / curvature
    new = old + step * (step * square - 2.0 * cross)
    coefs[0] = step
    coefs[1] = new / old

    for slot in range(1, 16):
        if slot < 8 or slot % 2:
            pass_on(0, slot, consumer).wait_send()
        give(slot, me).wait_send()

    @pl.when(upper == 0)
    def _():
        for slot in (8, 10, 12, 14):
            pass_on(0, slot, consumer).wait_send()

    for k in range(1, 8):
        share(0, st1, a_send, a_recv, k, me).wait_send()
    for m in range(1, GROUPS):
        share(1, st2, b_send, b_recv, m, me).wait_send()


def on_device(points, solution, residual, direction):
    vmem = pl.BlockSpec(memory_space=pltpu.VMEM)
    dma = pltpu.SemaphoreType.DMA
    image, coefs = pl.pallas_call(
        step_kernel,
        out_shape=(jax.ShapeDtypeStruct((R, W), f32), jax.ShapeDtypeStruct((2, R, W), f32)),
        in_specs=[pl.BlockSpec(memory_space=pltpu.HBM)] * 3,
        out_specs=(vmem, vmem),
        scratch_shapes=[
            pltpu.VMEM((F, W), bf16),
            pltpu.VMEM((R, W), f32),
            pltpu.VMEM((R, W), f32),
            pltpu.VMEM((16, ROWS, W), bf16),
            pltpu.VMEM((8, W, DEPTH), bf16),
            pltpu.VMEM((16, R, W), f32),
            pltpu.VMEM((2, W, W), bf16),
            pltpu.VMEM((16, R, W), f32),
            pltpu.VMEM((2, 8, 128), f32),
            pltpu.VMEM((8, 8, 128), f32),
            pltpu.VMEM((GROUPS, 8, 128), f32),
            dma((3,)), dma((16,)), dma((16,)), dma((16,)), dma((16,)),
            dma((8,)), dma((8,)), dma((GROUPS,)), dma((GROUPS,)),
        ],
        compiler_params=pltpu.CompilerParams(
            collective_id=0, has_side_effects=True, vmem_limit_bytes=67000000),
        name="cg_step",
    )(points, residual, direction)
    step, beta = coefs[0], coefs[1]
    residual_next = residual - step * image
    return (solution + step * direction, residual_next, residual_next + beta * direction)


def solution(mesh):
    placed = (P(None, ("row", "col")),) * 4
    return jax.shard_map(on_device, mesh=mesh, in_specs=placed, out_specs=placed[:3], check_vma=False)
```

```python
import math

import jax
import jax.numpy as jnp
from jax import lax
from jax.experimental import pallas as pl
from jax.experimental.pallas import tpu as pltpu
from jax.sharding import PartitionSpec as P

OFFSETS = ((0, 0), (0, 1), (1, 0), (3, 0), (2, 0), (2, 1), (1, 1), (3, 1))
SIBLING = 1
RELAYED = {2: 6, 3: 7, 4: 5}
SHIFT = ((2, 2), (1, 1), (1, 2), (3, 0), (2, 1), (0, 3), (0, 0), (1, 3))
F, R, W = 64, 16, 512
SENT = R + F
DEPTH = F + 16
ROWS = SENT + 16
GROUPS = 16
MESH = pl.DeviceIdType.MESH
bf16, f32 = jnp.bfloat16, jnp.float32


def step_kernel(points_hbm, residual_hbm, direction_hbm, image, coefs, points, residual, direction,
                blk, lhs, acc, k_even, k_odd, k_third, k_fourth, rs, stat, st1, st2,
                in_sem, g_send, g_recv, r_send, r_recv, a_send, a_recv, b_send, b_recv):
    loads = [pltpu.make_async_copy(src, dst, in_sem.at[n]) for n, (src, dst) in enumerate(
        ((points_hbm, points), (direction_hbm, direction), (residual_hbm, residual)))]
    for load in loads:
        load.start()

    row, col = lax.axis_index("row"), lax.axis_index("col")
    x, core = lax.rem(row, 4), lax.rem(col, 2)
    y, z = lax.rem(lax.div(col, 2), 2) * 2 + lax.div(row, 4), lax.div(col, 4)
    pos = x * 2 + core

    def beside(dev, k, sign=1):
        dx, dc = OFFSETS[k]
        there = lax.rem(x + (dx if sign > 0 else 4 - dx), 4) - x if dx else 0
        return (dev[0] + there, dev[1] + (dc * (1 - 2 * core) if dc else 0))

    def choose(values):
        return sum(jnp.where(pos == n, v, 0) for n, v in enumerate(values) if v)

    def moved(dy, dz):
        gy, gz = lax.rem(y + dy, 4), lax.rem(z + dz, 4)
        return (lax.rem(gy, 2) * 4 + x, gz * 4 + lax.div(gy, 2) * 2 + core)

    me = (row, col)
    turn = lax.rem(lax.div(y, 2) + lax.div(z, 2), 2)
    square = choose((0,) * 6 + (2, 0))
    shift_y, shift_z = choose([v[0] for v in SHIFT]), choose([v[1] for v in SHIFT])
    partner = moved(shift_y + square * (1 - turn), shift_z + square * turn)
    consumer = moved(4 - shift_y - square * turn, 4 - shift_z - square * (1 - turn))

    barrier = pltpu.get_barrier_semaphore()
    greeted = [beside(me, k) for k in (SIBLING, 2, 3, 4)] + [partner, consumer]
    for dev in greeted:
        pl.semaphore_signal(barrier, inc=1, device_id=dev, device_id_type=MESH)

    special = 1 - lax.div(pos + 7, 8)
    upper = special * lax.div(y, 2)
    lower = special - upper
    normal = 1 - special
    row_id = lax.broadcasted_iota(jnp.int32, (16, W), 0)

    def extend(slot):
        p = blk[slot, R:SENT, :].astype(f32)
        half = -0.5 * jnp.sum(p * p, axis=0, keepdims=True)
        hi = half.astype(bf16).astype(f32)
        mid = (half - hi).astype(bf16).astype(f32)
        lo = half - hi - mid
        pieces = jnp.where(row_id == 0, hi, jnp.where(row_id == 1, mid, jnp.where(row_id == 2, lo, 1.0)))
        blk[slot, SENT:ROWS, :] = jnp.where(row_id < 6, pieces, 0.0).astype(bf16)

    for load in loads:
        load.wait()
    blk[0, 0:R, :] = direction[...].astype(bf16)
    blk[0, R:SENT, :] = points[...]
    extend(0)
    acc[...] = jnp.zeros_like(acc)

    pl.semaphore_wait(barrier, len(greeted))

    def pass_on(src, dst, dev):
        return pltpu.make_async_remote_copy(
            src_ref=blk.at[src, pl.ds(0, SENT)], dst_ref=blk.at[dst, pl.ds(0, SENT)], send_sem=g_send.at[dst], recv_sem=g_recv.at[dst],
            device_id=dev, device_id_type=MESH)

    def forward(k):
        if k % 2:
            pass_on(k, 8 + k, consumer).start()
        else:
            @pl.when(upper == 0)
            def _():
                pass_on(k, 8 + k, consumer).start()

    forward(0)
    for k in (2, 3):
        pass_on(0, k, beside(me, k, -1)).start()
    pass_on(0, SIBLING, beside(me, SIBLING)).start()
    pass_on(0, 4, beside(me, 4)).start()

    def arrive(slot):
        pass_on(0, slot, consumer).wait_recv()
        extend(slot)

    def prepare(k):
        tail = pltpu.roll(blk[k, SENT:ROWS, :].astype(f32), 3, 0)
        tail = jnp.where(row_id < 3, 1.0, jnp.where(row_id < 6, tail, 0.0)).astype(bf16)
        lhs[k] = jnp.concatenate([blk[k, R:SENT, :], tail], axis=0).T

    def make(i, r, k_ref):
        s = jnp.dot(lhs[i], blk[r, R:ROWS, :], preferred_element_type=f32)
        k_ref[...] = jnp.exp2(s * (math.log2(math.e) / 16.0)).astype(bf16)

    def use_rows(i, r, k_ref):
        acc[i] += lax.dot_general(blk[r, 0:R, :], k_ref[...], (((1,), (1,)), ((), ())),
                                  preferred_element_type=f32)

    def use_columns(i, r, k_ref):
        acc[r] += jnp.dot(blk[i, 0:R, :], k_ref[...], preferred_element_type=f32)

    def own_block(k):
        arrive(k)
        if k in RELAYED:
            pass_on(k, RELAYED[k], beside(me, SIBLING)).start()

    near = (k_even, k_odd)
    prepare(0)
    make(0, 0, k_even)
    use_columns(0, 0, k_even)

    def tile(b, u):
        half, parity = lax.div(b, 2), lax.rem(b, 2)
        swap = special * (lax.div(b + 3, 16) - lax.div(b + 1, 16))
        half_s = half + swap * parity
        parity_s = parity + swap * (1 - 2 * parity)
        half_s = half_s - swap * (1 - parity)
        early, zero, last = 1 - lax.div(b + 13, 16), 1 - lax.div(b + 15, 16), lax.div(b + 1, 16)
        cross = early - zero
        i_n = cross * (8 - 2 * b + u % 2) + (1 - cross) * (4 * parity * (1 - last) + u)
        j_n = cross * (u // 2) + (1 - early) * ((1 - last) * lax.div(b + 1, 2) + last)
        hh, pair = lax.rem(half_s, 2), lax.div(half_s, 2)
        i_p = 4 * hh + upper * 2 * (u % 2) + (1 - upper) * u
        j_p = 2 * pair + upper * (u // 2) + (1 - upper)
        i_s = 4 * hh + u
        r_s = lax.rem(i_s + 1 + pair, 8)
        i = normal * i_n + special * ((1 - parity_s) * i_p + parity_s * i_s)
        r = normal * (8 + j_n) + special * ((1 - parity_s) * (8 + j_p) + parity_s * r_s)
        return i, r

    def give(slot, dev):
        return pltpu.make_async_remote_copy(
            src_ref=acc.at[slot], dst_ref=rs.at[slot], send_sem=r_send.at[slot], recv_sem=r_recv.at[slot],
            device_id=dev, device_id_type=MESH)

    def give_partner(j):
        give(8 + j, beside(partner, j)).start()

    def give_own(k):
        give(k, beside(me, k)).start()

    own_block(1)
    forward(1)
    prepare(1)
    for k in (2, 3):
        own_block(k)
    for k in (2, 3):
        forward(k)
        prepare(k)

    @pl.when(lower == 0)
    def _():
        arrive(8)

    @pl.when(special == 1)
    def _():
        arrive(9)

    def work(b, b_next, us):
        for u in us:
            make(*(tile(b, u + 1) if u < 3 else tile(b_next, 0)), near[(u + 1) % 2])
            i, r = tile(b, u)
            use_rows(i, r, near[u % 2])
            use_columns(i, r, near[u % 2])

    make(*tile(0, 0), k_even)
    work(0, 0, range(3))

    for k in (6, 7):
        own_block(k)
        prepare(k)

    work(0, 1, (3,))

    def arrivals(b):
        @pl.when(b == 1)
        def _():
            own_block(4)
            forward(4)
            prepare(4)

            @pl.when(special == 0)
            def _():
                arrive(9)

        @pl.when(b == 2)
        def _():
            own_block(5)
            prepare(5)
            for k in (5, 6, 7):
                forward(k)

        for j in range(2, 8):
            @pl.when(b == normal * (2 * j - 2) + special * (4 * (j // 2) - 1) + (0 if j % 2 else 100 * lower))
            def _():
                arrive(8 + j)

        for j, at in ((0, 4), (1, 5 + 100 * normal), (2, 7), (3, 8), (4, 11), (5, 12), (6, 14), (7, 14 + 100 * normal)):
            @pl.when(b == at)
            def _():
                give_partner(j)

        @pl.when(b + 100 * special == 14)
        def _():
            for k in (4, 5, 6, 7):
                give_own(k)

    def body(b, carry):
        arrivals(b)
        work(b, b + 1, range(4))
        return carry

    lax.fori_loop(1, 15, body, 0)

    @pl.when(special == 1)
    def _():
        for k in (4, 5, 6, 7):
            give_own(k)

    @pl.when(special == 0)
    def _():
        give_partner(7)
        spots = (k_even, k_odd, k_third, k_fourth)
        for u in range(4):
            if u < 3:
                make(*tile(15, u + 1), spots[u + 1])
            use_columns(*tile(15, u), spots[u])
        give_partner(1)
        for u in range(4):
            use_rows(*tile(15, u), spots[u])

    for k in (2, 3, 1):
        give_own(k)

    res, dirn = residual[...], direction[...]
    squares = jnp.sum(res * res, axis=1, keepdims=True)
    total = dirn + acc[0]
    for slot in (8, 10, 11, 12, 13, 14, 15, 6, 7, 4, 5, 1, 2, 3, 9):
        give(slot, me).wait_recv()
        total += rs[slot]
    image[...] = total

    sums = [squares] + [jnp.sum(v * total, axis=1, keepdims=True) for v in (dirn, res, total)]
    lane = lax.broadcasted_iota(jnp.int32, (8, 128), 1)
    packed = jnp.zeros((8, 128), f32)
    for n, v in enumerate(sums):
        packed = jnp.where(lane == n, v[0:8], jnp.where(lane == n + 4, v[8:16], packed))
    stat[0] = packed

    def share(src, dst, send, recv, m, dev):
        return pltpu.make_async_remote_copy(
            src_ref=stat.at[src], dst_ref=dst.at[m], send_sem=send.at[m], recv_sem=recv.at[m],
            device_id=dev, device_id_type=MESH)

    for k in (4, 5, 2, 3, 6, 7, 1):
        share(0, st1, a_send, a_recv, k, beside(me, k, -1)).start()
    ys = [lax.rem(y + d, 4) for d in range(4)]
    zs = [lax.rem(z + d, 4) * 4 for d in range(4)]
    rows = [lax.rem(v, 2) * 4 + x for v in ys]
    cols = [lax.div(v, 2) * 2 + core for v in ys]
    for k in (1, 2, 3, 6, 7, 4, 5):
        share(0, st1, a_send, a_recv, k, me).wait_recv()
        packed += st1[k]
    stat[1] = packed
    order = (10, 6, 14, 9, 11, 2, 8, 5, 7, 13, 15, 1, 3, 4, 12)
    for m in order:
        share(1, st2, b_send, b_recv, m, (rows[m // 4], cols[m // 4] + zs[m % 4])).start()
    for m in reversed(order):
        share(1, st2, b_send, b_recv, m, me).wait_recv()
        packed += st2[m]

    def pick(n):
        return jnp.concatenate([packed[:, n:n + 1], packed[:, n + 4:n + 5]], axis=0)

    old, curvature, cross, square = (pick(n) for n in range(4))
    step = old / curvature
    new = old + step * (step * square - 2.0 * cross)
    coefs[0] = jnp.broadcast_to(step, (R, W))
    coefs[1] = jnp.broadcast_to(new / old, (R, W))

    for slot in range(1, 16):
        if slot < 8 or slot % 2:
            pass_on(0, slot, consumer).wait_send()
        give(slot, me).wait_send()

    @pl.when(upper == 0)
    def _():
        for slot in (8, 10, 12, 14):
            pass_on(0, slot, consumer).wait_send()

    for k in range(1, 8):
        share(0, st1, a_send, a_recv, k, me).wait_send()
    for m in range(1, GROUPS):
        share(1, st2, b_send, b_recv, m, me).wait_send()


def on_device(points, solution, residual, direction):
    vmem = pl.BlockSpec(memory_space=pltpu.VMEM)
    dma = pltpu.SemaphoreType.DMA
    image, coefs = pl.pallas_call(
        step_kernel,
        out_shape=(jax.ShapeDtypeStruct((R, W), f32), jax.ShapeDtypeStruct((2, R, W), f32)),
        in_specs=[pl.BlockSpec(memory_space=pltpu.HBM)] * 3,
        out_specs=(vmem, vmem),
        scratch_shapes=[
            pltpu.VMEM((F, W), bf16),
            pltpu.VMEM((R, W), f32),
            pltpu.VMEM((R, W), f32),
            pltpu.VMEM((16, ROWS, W), bf16),
            pltpu.VMEM((8, W, DEPTH), bf16),
            pltpu.VMEM((16, R, W), f32),
            pltpu.VMEM((W, W), bf16),
            pltpu.VMEM((W, W), bf16),
            pltpu.VMEM((W, W), bf16),
            pltpu.VMEM((W, W), bf16),
            pltpu.VMEM((16, R, W), f32),
            pltpu.VMEM((2, 8, 128), f32),
            pltpu.VMEM((8, 8, 128), f32),
            pltpu.VMEM((GROUPS, 8, 128), f32),
            dma((3,)), dma((16,)), dma((16,)), dma((16,)), dma((16,)),
            dma((8,)), dma((8,)), dma((GROUPS,)), dma((GROUPS,)),
        ],
        compiler_params=pltpu.CompilerParams(
            collective_id=0, has_side_effects=True, vmem_limit_bytes=67000000),
        name="cg_step",
    )(points, residual, direction)
    step, beta = coefs[0], coefs[1]
    residual_next = residual - step * image
    return (solution + step * direction, residual_next, residual_next + beta * direction)


def solution(mesh):
    placed = (P(None, ("row", "col")),) * 4
    return jax.shard_map(on_device, mesh=mesh, in_specs=placed, out_specs=placed[:3], check_vma=False)
```

```python
import math

import jax
import jax.numpy as jnp
from jax import lax
from jax.experimental import pallas as pl
from jax.experimental.pallas import tpu as pltpu
from jax.sharding import PartitionSpec as P

OFFSETS = ((0, 0), (0, 1), (1, 0), (3, 0), (2, 0), (2, 1), (1, 1), (3, 1))
SIBLING = 1
RELAYED = {2: 6, 3: 7, 4: 5}
SHIFT = ((2, 2), (1, 1), (1, 2), (3, 0), (2, 1), (0, 3), (0, 0), (1, 3))
F, R, W = 64, 16, 512
SENT = R + F
DEPTH = F + 16
ROWS = SENT + 16
GROUPS = 16
MESH = pl.DeviceIdType.MESH
bf16, f32 = jnp.bfloat16, jnp.float32


def step_kernel(points_hbm, residual_hbm, direction_hbm, image, coefs, points, residual, direction,
                blk, lhs, acc, k_even, k_odd, k_third, k_fourth, rs, stat, st1, st2,
                in_sem, g_send, g_recv, r_send, r_recv, a_send, a_recv, b_send, b_recv):
    loads = [pltpu.make_async_copy(src, dst, in_sem.at[n]) for n, (src, dst) in enumerate(
        ((points_hbm, points), (direction_hbm, direction), (residual_hbm, residual)))]
    for load in loads:
        load.start()

    row, col = lax.axis_index("row"), lax.axis_index("col")
    x, core = lax.rem(row, 4), lax.rem(col, 2)
    y, z = lax.rem(lax.div(col, 2), 2) * 2 + lax.div(row, 4), lax.div(col, 4)
    pos = x * 2 + core

    def beside(dev, k, sign=1):
        dx, dc = OFFSETS[k]
        there = lax.rem(x + (dx if sign > 0 else 4 - dx), 4) - x if dx else 0
        return (dev[0] + there, dev[1] + (dc * (1 - 2 * core) if dc else 0))

    def choose(values):
        return sum(jnp.where(pos == n, v, 0) for n, v in enumerate(values) if v)

    def moved(dy, dz):
        gy, gz = lax.rem(y + dy, 4), lax.rem(z + dz, 4)
        return (lax.rem(gy, 2) * 4 + x, gz * 4 + lax.div(gy, 2) * 2 + core)

    me = (row, col)
    turn = lax.rem(lax.div(y, 2) + lax.div(z, 2), 2)
    square = choose((0,) * 6 + (2, 0))
    shift_y, shift_z = choose([v[0] for v in SHIFT]), choose([v[1] for v in SHIFT])
    partner = moved(shift_y + square * (1 - turn), shift_z + square * turn)
    consumer = moved(4 - shift_y - square * turn, 4 - shift_z - square * (1 - turn))

    barrier = pltpu.get_barrier_semaphore()
    greeted = [partner, consumer] + [beside(me, k) for k in (4, 2, 3, SIBLING)]
    for dev in greeted:
        pl.semaphore_signal(barrier, inc=1, device_id=dev, device_id_type=MESH)

    special = 1 - lax.div(pos + 7, 8)
    upper = special * lax.div(y, 2)
    lower = special - upper
    normal = 1 - special
    row_id = lax.broadcasted_iota(jnp.int32, (16, W), 0)

    def extend(slot):
        p = blk[slot, R:SENT, :].astype(f32)
        half = -0.5 * jnp.sum(p * p, axis=0, keepdims=True)
        hi = half.astype(bf16).astype(f32)
        mid = (half - hi).astype(bf16).astype(f32)
        lo = half - hi - mid
        pieces = jnp.where(row_id == 0, hi, jnp.where(row_id == 1, mid, jnp.where(row_id == 2, lo, 1.0)))
        blk[slot, SENT:ROWS, :] = jnp.where(row_id < 6, pieces, 0.0).astype(bf16)

    for load in loads:
        load.wait()
    blk[0, 0:R, :] = direction[...].astype(bf16)
    blk[0, R:SENT, :] = points[...]
    extend(0)
    acc[...] = jnp.zeros_like(acc)

    pl.semaphore_wait(barrier, len(greeted))

    def pass_on(src, dst, dev):
        return pltpu.make_async_remote_copy(
            src_ref=blk.at[src, pl.ds(0, SENT)], dst_ref=blk.at[dst, pl.ds(0, SENT)], send_sem=g_send.at[dst], recv_sem=g_recv.at[dst],
            device_id=dev, device_id_type=MESH)

    def forward(k):
        if k % 2:
            pass_on(k, 8 + k, consumer).start()
        else:
            @pl.when(upper == 0)
            def _():
                pass_on(k, 8 + k, consumer).start()

    forward(0)
    for k in (2, 3):
        pass_on(0, k, beside(me, k, -1)).start()
    pass_on(0, SIBLING, beside(me, SIBLING)).start()
    pass_on(0, 4, beside(me, 4)).start()

    def arrive(slot):
        pass_on(0, slot, consumer).wait_recv()
        extend(slot)

    def prepare(k):
        tail = pltpu.roll(blk[k, SENT:ROWS, :].astype(f32), 3, 0)
        tail = jnp.where(row_id < 3, 1.0, jnp.where(row_id < 6, tail, 0.0)).astype(bf16)
        lhs[k] = jnp.concatenate([blk[k, R:SENT, :], tail], axis=0).T

    def make(i, r, k_ref):
        s = jnp.dot(lhs[i], blk[r, R:ROWS, :], preferred_element_type=f32)
        k_ref[...] = jnp.exp2(s * (math.log2(math.e) / 16.0)).astype(bf16)

    def use_rows(i, r, k_ref):
        acc[i] += lax.dot_general(blk[r, 0:R, :], k_ref[...], (((1,), (1,)), ((), ())),
                                  preferred_element_type=f32)

    def use_columns(i, r, k_ref):
        acc[r] += jnp.dot(blk[i, 0:R, :], k_ref[...], preferred_element_type=f32)

    def own_block(k):
        arrive(k)
        if k in RELAYED:
            pass_on(k, RELAYED[k], beside(me, SIBLING)).start()

    near = (k_even, k_odd)
    prepare(0)
    make(0, 0, k_even)
    use_columns(0, 0, k_even)

    def tile(b, u):
        half, parity = lax.div(b, 2), lax.rem(b, 2)
        swap = special * (lax.div(b + 3, 16) - lax.div(b + 1, 16))
        half_s = half + swap * parity
        parity_s = parity + swap * (1 - 2 * parity)
        half_s = half_s - swap * (1 - parity)
        early, zero, last = 1 - lax.div(b + 13, 16), 1 - lax.div(b + 15, 16), lax.div(b + 1, 16)
        cross = early - zero
        i_n = cross * (8 - 2 * b + u % 2) + (1 - cross) * (4 * parity * (1 - last) + u)
        j_n = cross * (u // 2) + (1 - early) * ((1 - last) * lax.div(b + 1, 2) + last)
        hh, pair = lax.rem(half_s, 2), lax.div(half_s, 2)
        i_p = 4 * hh + upper * 2 * (u % 2) + (1 - upper) * u
        j_p = 2 * pair + upper * (u // 2) + (1 - upper)
        i_s = 4 * hh + u
        r_s = lax.rem(i_s + 1 + pair, 8)
        i = normal * i_n + special * ((1 - parity_s) * i_p + parity_s * i_s)
        r = normal * (8 + j_n) + special * ((1 - parity_s) * (8 + j_p) + parity_s * r_s)
        return i, r

    def give(slot, dev):
        return pltpu.make_async_remote_copy(
            src_ref=acc.at[slot], dst_ref=rs.at[slot], send_sem=r_send.at[slot], recv_sem=r_recv.at[slot],
            device_id=dev, device_id_type=MESH)

    def give_partner(j):
        give(8 + j, beside(partner, j)).start()

    def give_own(k):
        give(k, beside(me, k)).start()

    own_block(1)
    forward(1)
    prepare(1)
    for k in (2, 3):
        own_block(k)
    for k in (2, 3):
        forward(k)
        prepare(k)

    @pl.when(lower == 0)
    def _():
        arrive(8)

    @pl.when(special == 1)
    def _():
        arrive(9)

    def work(b, b_next, us):
        for u in us:
            make(*(tile(b, u + 1) if u < 3 else tile(b_next, 0)), near[(u + 1) % 2])
            i, r = tile(b, u)
            use_rows(i, r, near[u % 2])
            use_columns(i, r, near[u % 2])

    make(*tile(0, 0), k_even)
    work(0, 0, range(3))

    for k in (6, 7):
        own_block(k)
        prepare(k)

    work(0, 1, (3,))

    def arrivals(b):
        @pl.when(b == 1)
        def _():
            own_block(4)
            forward(4)
            prepare(4)

            @pl.when(special == 0)
            def _():
                arrive(9)

        @pl.when(b == 2)
        def _():
            own_block(5)
            prepare(5)
            for k in (5, 6, 7):
                forward(k)

        for j in range(2, 8):
            @pl.when(b == normal * (2 * j - 2) + special * (4 * (j // 2) - 1) + (0 if j % 2 else 100 * lower))
            def _():
                arrive(8 + j)

        for j, at in ((0, 4), (1, 5 + 100 * normal), (2, 7), (3, 8), (4, 11), (5, 12), (6, 14), (7, 14 + 100 * normal)):
            @pl.when(b == at)
            def _():
                give_partner(j)

        @pl.when(b + 100 * special == 14)
        def _():
            for k in (4, 5, 6, 7):
                give_own(k)

    def body(b, carry):
        arrivals(b)
        work(b, b + 1, range(4))
        return carry

    lax.fori_loop(1, 15, body, 0)

    @pl.when(special == 1)
    def _():
        for k in (4, 5, 6, 7):
            give_own(k)

    @pl.when(special == 0)
    def _():
        give_partner(7)
        spots = (k_even, k_odd, k_third, k_fourth)
        for u in range(4):
            if u < 3:
                make(*tile(15, u + 1), spots[u + 1])
            use_columns(*tile(15, u), spots[u])
        give_partner(1)
        for u in range(4):
            use_rows(*tile(15, u), spots[u])

    for k in (2, 3, 1):
        give_own(k)

    res, dirn = residual[...], direction[...]
    squares = jnp.sum(res * res, axis=1, keepdims=True)
    total = dirn + acc[0]
    for slot in (8, 10, 11, 12, 13, 14, 15, 6, 7, 4, 5, 1, 2, 3, 9):
        give(slot, me).wait_recv()
        total += rs[slot]
    image[...] = total

    sums = [squares] + [jnp.sum(v * total, axis=1, keepdims=True) for v in (dirn, res, total)]
    lane = lax.broadcasted_iota(jnp.int32, (8, 128), 1)
    packed = jnp.zeros((8, 128), f32)
    for n, v in enumerate(sums):
        packed = jnp.where(lane == n, v[0:8], jnp.where(lane == n + 4, v[8:16], packed))
    stat[0] = packed

    def share(src, dst, send, recv, m, dev):
        return pltpu.make_async_remote_copy(
            src_ref=stat.at[src], dst_ref=dst.at[m], send_sem=send.at[m], recv_sem=recv.at[m],
            device_id=dev, device_id_type=MESH)

    for k in (4, 5, 2, 3, 6, 7, 1):
        share(0, st1, a_send, a_recv, k, beside(me, k, -1)).start()
    ys = [lax.rem(y + d, 4) for d in range(4)]
    zs = [lax.rem(z + d, 4) * 4 for d in range(4)]
    rows = [lax.rem(v, 2) * 4 + x for v in ys]
    cols = [lax.div(v, 2) * 2 + core for v in ys]
    for k in (1, 2, 3, 6, 7, 4, 5):
        share(0, st1, a_send, a_recv, k, me).wait_recv()
        packed += st1[k]
    stat[1] = packed
    order = (10, 6, 14, 9, 11, 2, 8, 5, 7, 13, 15, 1, 3, 4, 12)
    for m in order:
        share(1, st2, b_send, b_recv, m, (rows[m // 4], cols[m // 4] + zs[m % 4])).start()
    for m in reversed(order):
        share(1, st2, b_send, b_recv, m, me).wait_recv()
        packed += st2[m]

    def pick(n):
        return jnp.concatenate([packed[:, n:n + 1], packed[:, n + 4:n + 5]], axis=0)

    old, curvature, cross, square = (pick(n) for n in range(4))
    step = old / curvature
    new = old + step * (step * square - 2.0 * cross)
    coefs[0] = jnp.broadcast_to(step, (R, W))
    coefs[1] = jnp.broadcast_to(new / old, (R, W))

    for slot in range(1, 16):
        if slot < 8 or slot % 2:
            pass_on(0, slot, consumer).wait_send()
        give(slot, me).wait_send()

    @pl.when(upper == 0)
    def _():
        for slot in (8, 10, 12, 14):
            pass_on(0, slot, consumer).wait_send()

    for k in range(1, 8):
        share(0, st1, a_send, a_recv, k, me).wait_send()
    for m in range(1, GROUPS):
        share(1, st2, b_send, b_recv, m, me).wait_send()


def on_device(points, solution, residual, direction):
    vmem = pl.BlockSpec(memory_space=pltpu.VMEM)
    dma = pltpu.SemaphoreType.DMA
    image, coefs = pl.pallas_call(
        step_kernel,
        out_shape=(jax.ShapeDtypeStruct((R, W), f32), jax.ShapeDtypeStruct((2, R, W), f32)),
        in_specs=[pl.BlockSpec(memory_space=pltpu.HBM)] * 3,
        out_specs=(vmem, vmem),
        scratch_shapes=[
            pltpu.VMEM((F, W), bf16),
            pltpu.VMEM((R, W), f32),
            pltpu.VMEM((R, W), f32),
            pltpu.VMEM((16, ROWS, W), bf16),
            pltpu.VMEM((8, W, DEPTH), bf16),
            pltpu.VMEM((16, R, W), f32),
            pltpu.VMEM((W, W), bf16),
            pltpu.VMEM((W, W), bf16),
            pltpu.VMEM((W, W), bf16),
            pltpu.VMEM((W, W), bf16),
            pltpu.VMEM((16, R, W), f32),
            pltpu.VMEM((2, 8, 128), f32),
            pltpu.VMEM((8, 8, 128), f32),
            pltpu.VMEM((GROUPS, 8, 128), f32),
            dma((3,)), dma((16,)), dma((16,)), dma((16,)), dma((16,)),
            dma((8,)), dma((8,)), dma((GROUPS,)), dma((GROUPS,)),
        ],
        compiler_params=pltpu.CompilerParams(
            collective_id=0, has_side_effects=True, vmem_limit_bytes=67000000),
        name="cg_step",
    )(points, residual, direction)
    step, beta = coefs[0], coefs[1]
    residual_next = residual - step * image
    return (solution + step * direction, residual_next, residual_next + beta * direction)


def solution(mesh):
    placed = (P(None, ("row", "col")),) * 4
    return jax.shard_map(on_device, mesh=mesh, in_specs=placed, out_specs=placed[:3], check_vma=False)
```
